32 devices in a mesh: dp: 8 (over z, y), tensor: 4 (over x, core).
Axes of the slice: x: 2, y: 2, z: 4, core: 2. Of those that a mesh axis runs over, the one named last changes fastest.
Arguments:
- layer_in: bfloat16 [16, 512, 768], P('dp'), may hold values from -6 to 6
- cotangent: bfloat16 [16, 512, 768], P('dp'), may hold values from -6 to 6
- seq_lengths: int32 [16], P('dp'), may hold values from 128 to 512, as said below
- labels: int32 [16], P('dp'), may hold values from 0 to 2
- w_qkv: bfloat16 [768, 3, 768], P('dp', None, 'tensor'), may hold values from -0.21875 to 0.21875
- b_q: float32 [768], P('tensor'), may hold values from -3 to 3
- b_v: float32 [768], P('tensor'), may hold values from -3 to 3
- w_out: bfloat16 [768, 768], P('tensor', 'dp'), may hold values from -1.75 to 1.75
- b_out: float32 [768], replicated, may hold values from -3 to 3
- ln1_gain: float32 [768], replicated, may hold values from 0.5 to 1.5
- ln1_bias: float32 [768], replicated, may hold values from -2 to 2
- w_up: bfloat16 [768, 3072], P('dp', 'tensor'), may hold values from -0.21875 to 0.21875
- b_up: float32 [3072], P('tensor'), may hold values from -3 to 3
- w_down: bfloat16 [3072, 768], P('tensor', 'dp'), may hold values from -0.109375 to 0.109375
- b_down: float32 [768], replicated, may hold values from -3 to 3
- ln2_gain: float32 [768], replicated, may hold values from 0.5 to 1.5
- ln2_bias: float32 [768], replicated, may hold values from -2 to 2
- pool_w: float32 [768, 768], replicated, may hold values from -0.21875 to 0.21875
- pool_b: float32 [768], replicated, may hold values from -3 to 3
- class_w: float32 [768, 3], replicated, may hold values from -0.625 to 0.625
- class_b: float32 [3], replicated, may hold values from -3 to 3
Outputs:
- layer_out: bfloat16 [16, 512, 768], P('dp')
- input_grad: bfloat16 [16, 512, 768], P('dp')
- ramp_loss: float32 [], replicated
- grad_w_qkv: float32 [768, 3, 768], P('dp', None, 'tensor')
- grad_b_q: float32 [768], P('tensor')
- grad_b_v: float32 [768], P('tensor')
- grad_w_out: float32 [768, 768], P('tensor', 'dp')
- grad_b_out: float32 [768], replicated
- grad_ln1_gain: float32 [768], replicated
- grad_ln1_bias: float32 [768], replicated
- grad_w_up: float32 [768, 3072], P('dp', 'tensor')
- grad_b_up: float32 [3072], P('tensor')
- grad_w_down: float32 [3072, 768], P('tensor', 'dp')
- grad_b_down: float32 [768], replicated
- grad_ln2_gain: float32 [768], replicated
- grad_ln2_bias: float32 [768], replicated
- grad_pool_w: float32 [768, 768], replicated
- grad_pool_b: float32 [768], replicated
- grad_class_w: float32 [768, 3], replicated
- grad_class_b: float32 [3], replicated
The draws below stay inside these ranges and needn't reach their ends.
Inputs may be any that keep to these rules, and one draw needn't show every extreme that they name: `seq_lengths`: each sequence's valid tokens form a prefix; at least one sequence is full and at least one has 128 tokens.
All inputs are finite; a program needn't handle non-finite values.
Results may differ from the reference program's by a relative error of at most 0.018.
Values may be sent and summed in bfloat16 or wider, within the bound.
No kernel may reach another device: no remote copies, remote signals or barrier semaphores. Data moves between devices by JAX's collectives and lax.ppermute only.
A program may use at most 128 MiB of HBM per device.

```python
from functools import partial
import jax
import jax.numpy as jnp
from jax import lax

D = 768
HEADS = 12
HEAD_DIM = 64
FF = 3072
CLASSES = 3
LEN = 512
SEQS = 16


def draw_seq_lengths(key, part):
    picks = jax.random.randint(key, (SEQS,), 0, LEN + 1)
    result = LEN // 4 + 3 * picks * picks // (4 * LEN)
    result = result.at[0].set(LEN).at[1].set(LEN // 4)
    return result.astype(jnp.int32)


def set_ends(values, key, smallest, top_value):
    index_at = [jax.random.randint(jax.random.fold_in(key, axis), (), 0, length) for axis, length in enumerate(values.shape)]
    main_axis = values.shape.index(max(values.shape))
    next_to = index_at[:main_axis] + [(index_at[main_axis] + 1) % values.shape[main_axis]] + index_at[main_axis + 1:]
    return values.at[tuple(index_at)].set(smallest).at[tuple(next_to)].set(top_value)


def shard_levels(own_key, shape, cuts, low, top_value):
    factor_of, own = 1.0, jax.random.fold_in(own_key, 6)
    for axis_at, parts in cuts:
        steps = jnp.exp(jax.random.uniform(jax.random.fold_in(own, axis_at), (parts,), jnp.float32, low / len(cuts), top_value / len(cuts)))
        factor_of = factor_of * jnp.repeat(steps, shape[axis_at] // parts).reshape([-1 if axis == axis_at else 1 for axis in range(len(shape))])
    return factor_of


def bell_draw(rng, shape, deviation, bound, cuts=(), kind=jnp.bfloat16):
    array = deviation * jax.random.normal(rng, shape, jnp.float32)
    if cuts:
        array = array * shard_levels(rng, shape, cuts, -0.22, 0.18)
    return jnp.clip(array, -bound, bound).astype(kind)


def setup_inputs(seed: int = 0) -> dict:
    streams_of = jax.random.split(jax.random.key(seed), 22)
    layer_in = bell_draw(streams_of[0], (SEQS, LEN, D), 1.0, 6.0, ((0, 8),))
    cotangent = bell_draw(streams_of[1], (SEQS, LEN, D), 1.0, 6.0, ((0, 8),))
    seq_lengths = draw_seq_lengths(jax.random.fold_in(streams_of[21], 71), 0)
    labels = set_ends(jax.random.randint(streams_of[3], (SEQS,), 0, CLASSES), jax.random.fold_in(streams_of[3], 1), 0, CLASSES - 1).astype(jnp.int32)
    w_qkv = bell_draw(streams_of[4], (D, 3, D), D ** -0.5, 0.21875, ((0, 8), (2, 4)))
    b_q = bell_draw(streams_of[5], (D,), 0.5, 3.0, ((0, 4),), jnp.float32)
    b_v = bell_draw(streams_of[6], (D,), 0.5, 3.0, ((0, 4),), jnp.float32)
    w_out = bell_draw(streams_of[7], (D, D), (D // 64) ** -0.5, 1.75, ((0, 4), (1, 8)))
    b_out = bell_draw(streams_of[8], (D,), 0.5, 3.0, (), jnp.float32)
    ln1_gain = jnp.clip(1.0 + 0.1 * jax.random.normal(streams_of[9], (D,), jnp.float32), 0.5, 1.5)
    ln1_bias = bell_draw(streams_of[10], (D,), 0.3, 2.0, (), jnp.float32)
    w_up = bell_draw(streams_of[11], (D, FF), D ** -0.5, 0.21875, ((0, 8), (1, 4)))
    b_up = bell_draw(streams_of[12], (FF,), 0.5, 3.0, ((0, 4),), jnp.float32)
    w_down = bell_draw(streams_of[13], (FF, D), FF ** -0.5, 0.109375, ((0, 4), (1, 8)))
    b_down = bell_draw(streams_of[14], (D,), 0.5, 3.0, (), jnp.float32)
    ln2_gain = jnp.clip(1.0 + 0.1 * jax.random.normal(streams_of[15], (D,), jnp.float32), 0.5, 1.5)
    ln2_bias = bell_draw(streams_of[16], (D,), 0.3, 2.0, (), jnp.float32)
    pool_w = bell_draw(streams_of[17], (D, D), D ** -0.5, 0.21875, (), jnp.float32)
    pool_b = bell_draw(streams_of[18], (D,), 0.5, 3.0, (), jnp.float32)
    class_w = bell_draw(streams_of[19], (D, CLASSES), (D // 8) ** -0.5, 0.625, (), jnp.float32)
    class_b = bell_draw(streams_of[20], (CLASSES,), 1.0, 3.0, (), jnp.float32)
    return dict(layer_in=layer_in, cotangent=cotangent, seq_lengths=seq_lengths, labels=labels, w_qkv=w_qkv, b_q=b_q, b_v=b_v, w_out=w_out, b_out=b_out, ln1_gain=ln1_gain, ln1_bias=ln1_bias, w_up=w_up, b_up=b_up, w_down=w_down, b_down=b_down, ln2_gain=ln2_gain, ln2_bias=ln2_bias, pool_w=pool_w, pool_b=pool_b, class_w=class_w, class_b=class_b)


@jax.custom_vjp
def low(v):
    return lax.optimization_barrier(v.astype(jnp.bfloat16)).astype(jnp.float32)

@jax.custom_vjp
def low_back(v):
    return v

def low_keep(v):
    return (low(v), None)

def low_pass(kept, grad):
    return (grad,)

def back_keep(v):
    return (v, None)

def back_low(kept, grad):
    return (low(grad),)
low.defvjp(low_keep, low_pass)
low_back.defvjp(back_keep, back_low)
norm_eps = 1e-12

def layer_norm(values, gain, shift):
    center = values - lax.optimization_barrier(jnp.mean(values, axis=-1, keepdims=True))
    spread = lax.optimization_barrier(jnp.mean(center * center, axis=-1, keepdims=True))
    return center * lax.rsqrt(spread + norm_eps) * gain + shift

def forward(params, x_group, cot_group, seq_lens, seq_labels):
    w_qkv, b_q, b_v, w_out, b_out, ln1_gain, ln1_bias, w_up, b_up, w_down, b_down, ln2_gain, ln2_bias, pool_w, pool_b, class_w, class_b = params
    highest = lax.Precision.HIGHEST
    group_size, seq_span = (x_group.shape[0], x_group.shape[1])
    qkv_proj = jnp.einsum('gld,dcf->glcf', x_group, w_qkv, precision=highest)
    q_heads = low_back(low(qkv_proj[:, :, 0] + b_q)).reshape(group_size, seq_span, HEADS, HEAD_DIM)
    k_heads = low_back(low(qkv_proj[:, :, 1])).reshape(group_size, seq_span, HEADS, HEAD_DIM)
    v_heads = low_back(low(qkv_proj[:, :, 2] + b_v)).reshape(group_size, seq_span, HEADS, HEAD_DIM)
    positions = jnp.arange(seq_span)
    valid = positions[None, :] < seq_lens[:, None]
    key_bias = jnp.where(valid, 0.0, -1000000000.0).astype(jnp.float32)
    scores = jnp.einsum('gqhe,gkhe->ghqk', q_heads, k_heads, precision=highest) * 0.125
    scores = low_back(scores + key_bias[:, None, None, :])
    attn_probs = jax.nn.softmax(scores, axis=-1)
    context = jnp.einsum('ghqk,gkhe->gqhe', low(attn_probs), v_heads, precision=highest)
    context = low_back(low(context.reshape(group_size, seq_span, D)))
    attn_out = low_back(jnp.einsum('gld,de->gle', context, w_out, precision=highest))
    normed_mid = layer_norm(x_group + attn_out + b_out, ln1_gain, ln1_bias)
    pre_act = low_back(jnp.einsum('gld,df->glf', low(normed_mid), w_up, precision=highest) + b_up)
    post_act = low(jax.nn.gelu(pre_act, approximate=False))
    ffn_out = low_back(jnp.einsum('glf,fd->gld', post_act, w_down, precision=highest))
    row_mask = valid.astype(jnp.float32)[:, :, None]
    layer_output = layer_norm(normed_mid + ffn_out + b_down, ln2_gain, ln2_bias) * row_mask
    first_tok = layer_output[:, 0]
    pooled = jnp.tanh(jnp.dot(first_tok, pool_w, precision=highest) + pool_b)
    logits = jnp.dot(pooled, class_w, precision=highest) + class_b
    onehot = (seq_labels[:, None] == jnp.arange(CLASSES)[None, :]).astype(jnp.float32)
    losses = jax.nn.logsumexp(logits, axis=-1) - lax.optimization_barrier(jnp.sum(onehot * logits, axis=-1))
    objective = jnp.sum(layer_output * cot_group) + jnp.sum(losses)
    return (objective, (layer_output, losses))

def reference(layer_in, cotangent, seq_lengths, labels, w_qkv, b_q, b_v, w_out, b_out, ln1_gain, ln1_bias, w_up, b_up, w_down, b_down, ln2_gain, ln2_bias, pool_w, pool_b, class_w, class_b):
    params = tuple((p.astype(jnp.float32) for p in (w_qkv, b_q, b_v, w_out, b_out, ln1_gain, ln1_bias, w_up, b_up, w_down, b_down, ln2_gain, ln2_bias, pool_w, pool_b, class_w, class_b)))
    group_size = 8
    group_count = SEQS // group_size
    scan_items = (layer_in.reshape(group_count, group_size, LEN, D), cotangent.reshape(group_count, group_size, LEN, D), seq_lengths.reshape(group_count, group_size), labels.reshape(group_count, group_size))

    def step(running, current):
        x_group, cot_group, len_group, lab_group = current
        objective, pullback, aux_out = jax.vjp(partial(forward, cot_group=cot_group.astype(jnp.float32), seq_lens=len_group, seq_labels=lab_group), params, x_group.astype(jnp.float32), has_aux=True)
        gradients, grad_in = pullback(jnp.ones_like(objective))
        running = jax.tree.map(jnp.add, running, gradients)
        return (running, (aux_out[0].astype(jnp.bfloat16), grad_in.astype(jnp.bfloat16), aux_out[1]))
    init = jax.tree.map(jnp.zeros_like, params)
    sums, (outputs, in_grads, losses) = lax.scan(step, init, scan_items)
    g_qkv, g_bq, g_bv, g_out, g_bout, g_g1, g_s1, g_up, g_bup, g_down, g_bdown, g_g2, g_s2, g_pw, g_pb, g_cw, g_cb = sums
    return (outputs.reshape(SEQS, LEN, D), in_grads.reshape(SEQS, LEN, D), jnp.mean(losses), g_qkv, g_bq, g_bv, g_out, g_bout, g_g1, g_s1, g_up, g_bup, g_down, g_bdown, g_g2, g_s2, g_pw, g_pb, g_cw, g_cb)
```

```python
import math

import jax
import jax.numpy as jnp
from jax import lax
from jax.sharding import PartitionSpec as P

HEAD_DIM = 64
CLASSES = 3
CHUNKS = 2
EPS = 1e-12
F32 = jnp.float32
BF16 = jnp.bfloat16
highest = lax.Precision.HIGHEST


def nn(a, b):
    return lax.dot_general(a, b, (((1,), (0,)), ((), ())), preferred_element_type=F32)


def nt(a, b):
    return lax.dot_general(a, b, (((1,), (1,)), ((), ())), preferred_element_type=F32)


def tn(a, b):
    return lax.dot_general(a, b, (((0,), (0,)), ((), ())), preferred_element_type=F32)


def local(
    layer_in,
    cotangent,
    seq_lengths,
    labels,
    w_qkv,
    b_q,
    b_v,
    w_out,
    b_out,
    ln1_gain,
    ln1_bias,
    w_up,
    b_up,
    w_down,
    b_down,
    ln2_gain,
    ln2_bias,
    pool_w,
    pool_b,
    class_w,
    class_b,
):
    share, span, width = layer_in.shape
    dp = lax.axis_size("dp")
    tensor = lax.axis_size("tensor")
    high = dp // 2
    qw = b_q.shape[0]
    ff = b_up.shape[0]
    rows_w = w_up.shape[0]
    att = 4 * qw
    t_idx = lax.axis_index("tensor")
    core = lax.rem(t_idx, share)
    y_idx = lax.rem(lax.axis_index("dp"), 2)

    core_pairs = [(i, i ^ 1) for i in range(tensor)]
    x_pairs = [(i, i ^ 2) for i in range(tensor)]
    y_pairs = [(i, i ^ 1) for i in range(dp)]
    z_groups = [list(range(j, dp, 2)) for j in range(2)]

    def to_core(a):
        return lax.ppermute(a, "tensor", core_pairs)

    def over_x(a):
        return lax.ppermute(a, "tensor", x_pairs)

    def over_y(a):
        return lax.ppermute(a, "dp", y_pairs)

    def over_z(a):
        return lax.all_to_all(a, "dp", 0, 0, tiled=True, axis_index_groups=z_groups)

    def gather(shard):
        rows, cols = shard.shape
        mine = over_z(jnp.tile(shard, (high, 1))).reshape(high, 1, rows, cols)
        theirs = over_y(mine)
        even = jnp.concatenate([mine, theirs], axis=1)
        odd = jnp.concatenate([theirs, mine], axis=1)
        own = jnp.where(y_idx == 0, even, odd).reshape(dp * rows, cols)
        return own, to_core(own)

    def scatter(grad):
        rows, cols = grad.shape
        parts = grad.reshape(high, 2, rows // dp, cols)
        keep = jnp.where(y_idx == 0, parts[:, 0], parts[:, 1])
        give = jnp.where(y_idx == 0, parts[:, 1], parts[:, 0])
        got = over_y(give.astype(BF16))
        half = (keep + got.astype(F32)).astype(BF16)
        out = over_z(half.reshape(high * rows // dp, cols)).reshape(high, rows // dp, cols)
        return jnp.sum(out.astype(F32), axis=0)

    shard_att = jnp.concatenate([w_qkv.reshape(rows_w, 3 * qw), w_out.T], axis=1)
    shard_ffn = jnp.concatenate([w_up, w_down.T], axis=1)
    att_own, att_oth = gather(shard_att)
    ffn_own, ffn_oth = gather(shard_ffn)
    bias_own = jnp.concatenate([b_q, b_v, b_up])
    bias_oth = to_core(bias_own)
    bq, bv, bup = (
        jnp.concatenate([bias_own[a:b], bias_oth[a:b]])
        for a, b in ((0, qw), (qw, 2 * qw), (2 * qw, 2 * qw + ff))
    )

    pick = lambda a: lax.dynamic_index_in_dim(a, core, 0, keepdims=False)
    x = pick(layer_in)
    cot = pick(cotangent)
    length = pick(seq_lengths)
    label = pick(labels)

    p_own = nn(x, att_own[:, : 3 * qw])
    p_oth = nn(x, att_oth[:, : 3 * qw])
    q = (jnp.concatenate([p_own[:, :qw], p_oth[:, :qw]], 1) + bq).astype(BF16)
    k = jnp.concatenate([p_own[:, qw : 2 * qw], p_oth[:, qw : 2 * qw]], 1).astype(BF16)
    v = (jnp.concatenate([p_own[:, 2 * qw :], p_oth[:, 2 * qw :]], 1) + bv).astype(BF16)
    heads = 2 * qw // HEAD_DIM
    wo_own, wo_oth = att_own[:, 3 * qw :], att_oth[:, 3 * qw :]
    split = lambda a: a.reshape(a.shape[0], heads, HEAD_DIM)
    k3, v3 = split(k), split(v)
    key_bias = jnp.where(jnp.arange(span) < length, 0.0, -1e9).astype(F32)

    step = span // CHUNKS
    cuts = [slice(i * step, (i + 1) * step) for i in range(CHUNKS)]

    def scores_of(rows):
        s = jnp.einsum("qhe,khe->hqk", split(q[rows]), k3, preferred_element_type=F32)
        return s * 0.125 + key_bias

    ctx, lse, part = [], [], []
    for rows in cuts:
        s = scores_of(rows)
        top = jnp.max(s, -1, keepdims=True)
        l = top + jnp.log(jnp.sum(jnp.exp(s - top), -1, keepdims=True))
        p = jnp.exp(s - l).astype(BF16)
        c = jnp.einsum("hqk,khe->qhe", p, v3, preferred_element_type=F32)
        c = c.reshape(step, 2 * qw).astype(BF16)
        ctx.append(c)
        lse.append(l)
        part.append((nt(c[:, :qw], wo_own) + nt(c[:, qw:], wo_oth)).astype(BF16))
    recv = [over_x(a) for a in part]

    hat1, rstd1, mid_b, post, slope, fpart = [], [], [], [], [], []
    up_own, up_oth = ffn_own[:, :ff], ffn_oth[:, :ff]
    dn_own, dn_oth = ffn_own[:, ff:], ffn_oth[:, ff:]
    for i, rows in enumerate(cuts):
        r = x[rows].astype(F32) + (part[i].astype(F32) + recv[i].astype(F32)) + b_out
        cen = r - jnp.mean(r, -1, keepdims=True)
        rs = lax.rsqrt(jnp.mean(cen * cen, -1, keepdims=True) + EPS)
        h = cen * rs
        m = (h * ln1_gain + ln1_bias).astype(BF16)
        pre = jnp.concatenate([nn(m, up_own), nn(m, up_oth)], 1) + bup
        cdf = 0.5 * (1.0 + lax.erf(pre * math.sqrt(0.5)))
        pdf = jnp.exp(-0.5 * pre * pre) * (1.0 / math.sqrt(2.0 * math.pi))
        po = (pre * cdf).astype(BF16)
        hat1.append(h)
        rstd1.append(rs)
        mid_b.append(m)
        post.append(po)
        slope.append((cdf + pre * pdf).astype(BF16))
        fpart.append((nt(po[:, :ff], dn_own) + nt(po[:, ff:], dn_oth)).astype(BF16))
    frecv = [over_x(a) for a in fpart]

    outs, g_res2, g_ffn, g_pre, mpart = [], [], [], [], []
    ramp = None
    small2 = 0.0
    small_up = 0.0
    for i, rows in enumerate(cuts):
        mid = hat1[i] * ln1_gain + ln1_bias
        r = mid + (fpart[i].astype(F32) + frecv[i].astype(F32)) + b_down
        cen = r - jnp.mean(r, -1, keepdims=True)
        rs = lax.rsqrt(jnp.mean(cen * cen, -1, keepdims=True) + EPS)
        h = cen * rs
        mask = (jnp.arange(step) + rows.start < length).astype(F32)[:, None]
        normed = (h * ln2_gain + ln2_bias) * mask
        outs.append(normed.astype(BF16))
        g = cot[rows].astype(F32)
        if i == 0:
            first = normed[:1]
            pooled = jnp.tanh(jnp.dot(first, pool_w, precision=highest) + pool_b)
            logits = jnp.dot(pooled, class_w, precision=highest) + class_b
            onehot = (jnp.arange(CLASSES) == label).astype(F32)[None]
            big = jax.nn.logsumexp(logits, axis=-1, keepdims=True)
            ce = big - jnp.sum(onehot * logits, -1, keepdims=True)
            d_log = jnp.exp(logits - big) - onehot
            d_pool = jnp.dot(d_log, class_w.T, precision=highest)
            d_z = d_pool * (1.0 - pooled * pooled)
            d_first = jnp.dot(d_z, pool_w.T, precision=highest)
            g = g.at[0].add(d_first[0])
            tail = jnp.concatenate([d_log, ce, jnp.zeros((1, width - CLASSES - 1), F32)], 1)
            ramp = jnp.concatenate([first, d_z, pooled, tail], 0)
        g = g * mask
        gh = g * ln2_gain
        gr = rs * (
            gh - jnp.mean(gh, -1, keepdims=True) - h * jnp.mean(gh * h, -1, keepdims=True)
        )
        small2 = small2 + jnp.stack([jnp.sum(gr, 0), jnp.sum(g * h, 0), jnp.sum(g, 0)])
        gf = gr.astype(BF16)
        g_post = jnp.concatenate([nn(gf, dn_own), nn(gf, dn_oth)], 1)
        gp = (g_post * slope[i].astype(F32)).astype(BF16)
        small_up = small_up + jnp.sum(gp.astype(F32), 0)
        g_res2.append(gr)
        g_ffn.append(gf)
        g_pre.append(gp)
        mpart.append((nt(gp[:, :ff], up_own) + nt(gp[:, ff:], up_oth)).astype(BF16))
    mrecv = [over_x(a) for a in mpart]

    join = lambda a: jnp.concatenate(a, 0)
    mid_all, post_all, gffn_all, gpre_all = join(mid_b), join(post), join(g_ffn), join(g_pre)
    o_mid = to_core(mid_all)
    o_post = to_core(post_all[:, ff:])
    o_gffn = to_core(gffn_all)
    o_gpre = to_core(gpre_all[:, ff:])
    grad_up = tn(join([mid_all, o_mid]), join([gpre_all[:, :ff], o_gpre]))
    grad_dn = tn(join([gffn_all, o_gffn]), join([post_all[:, :ff], o_post]))
    red_ffn = scatter(jnp.concatenate([grad_up, grad_dn], 1))

    g_res1, g_attn, dq = [], [], []
    dk = dv = 0.0
    small1 = 0.0
    for i, rows in enumerate(cuts):
        g = g_res2[i] + (mpart[i].astype(F32) + mrecv[i].astype(F32))
        h = hat1[i]
        gh = g * ln1_gain
        gr = rstd1[i] * (
            gh - jnp.mean(gh, -1, keepdims=True) - h * jnp.mean(gh * h, -1, keepdims=True)
        )
        small1 = small1 + jnp.stack([jnp.sum(gr, 0), jnp.sum(g * h, 0), jnp.sum(g, 0)])
        ga = gr.astype(BF16)
        gc = jnp.concatenate([nn(ga, wo_own), nn(ga, wo_oth)], 1).astype(BF16)
        gc3 = split(gc)
        p = jnp.exp(scores_of(rows) - lse[i])
        dv = dv + jnp.einsum("hqk,qhe->khe", p.astype(BF16), gc3, preferred_element_type=F32)
        gp = jnp.einsum("qhe,khe->hqk", gc3, v3, preferred_element_type=F32)
        ds = (p * (gp - jnp.sum(p * gp, -1, keepdims=True))).astype(BF16)
        dq_i = jnp.einsum("hqk,khe->qhe", ds, k3, preferred_element_type=F32) * 0.125
        dk = dk + jnp.einsum("hqk,qhe->khe", ds, split(q[rows]), preferred_element_type=F32)
        dq.append(dq_i.reshape(step, 2 * qw).astype(BF16))
        g_res1.append(gr)
        g_attn.append(ga)
    dq = join(dq)
    dk = (dk * 0.125).reshape(span, 2 * qw).astype(BF16)
    dv = dv.reshape(span, 2 * qw).astype(BF16)
    gp_own = jnp.concatenate([dq[:, :qw], dk[:, :qw], dv[:, :qw]], 1)
    gp_oth = jnp.concatenate([dq[:, qw:], dk[:, qw:], dv[:, qw:]], 1)
    ipart = [
        (nt(gp_own[r], att_own[:, : 3 * qw]) + nt(gp_oth[r], att_oth[:, : 3 * qw])).astype(BF16)
        for r in cuts
    ]
    irecv = [over_x(a) for a in ipart]

    ctx_all, ga_all = join(ctx), join(g_attn)
    o_ctx = to_core(ctx_all[:, qw:])
    o_ga = to_core(ga_all)
    o_gp = to_core(gp_oth)
    x_oth = lax.dynamic_index_in_dim(layer_in, 1 - core, 0, keepdims=False)
    grad_qkv = tn(join([x, x_oth]), join([gp_own, o_gp]))
    grad_out = tn(join([ga_all, o_ga]), join([ctx_all[:, :qw], o_ctx]))
    red_att = scatter(jnp.concatenate([grad_qkv, grad_out], 1))

    sq = jnp.sum(dq.astype(F32), 0)
    sv = jnp.sum(dv.astype(F32), 0)
    pad = jnp.zeros((width - 2 * qw,), F32)
    common = jnp.concatenate([small1, small2], 0)
    line = lambda s: jnp.concatenate([sq[s], sv[s], pad])[None]
    upper = small_up.reshape(2, ff)
    mine = jnp.concatenate([common, line(slice(0, qw)), upper[:1], ramp], 0)
    send = jnp.concatenate([common, line(slice(qw, None)), upper[1:], ramp], 0)
    other = to_core(send)
    n_sum = common.shape[0] + 2
    flip = lambda a, b: jnp.where(core == 0, jnp.concatenate([a, b], 0), jnp.concatenate([b, a], 0))
    pack = jnp.concatenate([mine[:n_sum] + other[:n_sum], flip(mine[n_sum:], other[n_sum:])], 0)
    pack = lax.all_to_all(jnp.tile(pack[None], (dp, 1, 1)), "dp", 0, 0, tiled=True)
    total = jnp.sum(pack[:, :n_sum], axis=0)
    ramps = pack[:, n_sum:].reshape(dp * share, 4, width)
    f_all, z_all, p_all, t_all = (ramps[:, j] for j in range(4))
    d_all = t_all[:, :CLASSES]
    tdot = lambda a, b: lax.dot_general(a, b, (((0,), (0,)), ((), ())), precision=highest)
    g_pw = tdot(f_all, z_all)
    g_cw = tdot(p_all, d_all)
    loss = jnp.sum(t_all[:, CLASSES]) / (dp * share)

    both = lambda mine_, other_: jnp.where(
        core == 0, jnp.stack([mine_, other_]), jnp.stack([other_, mine_])
    )
    out = join(outs)
    layer_out = both(out, to_core(out))
    gin = join(
        [
            (g_res1[i] + (ipart[i] + irecv[i]).astype(F32)).astype(BF16)
            for i in range(CHUNKS)
        ]
    )
    input_grad = both(gin, to_core(gin))
    return (
        layer_out,
        input_grad,
        loss,
        red_att[:, : 3 * qw].reshape(rows_w, 3, qw),
        total[6, :qw],
        total[6, qw : 2 * qw],
        red_att[:, 3 * qw :].T,
        total[0],
        total[1],
        total[2],
        red_ffn[:, :ff],
        total[7],
        red_ffn[:, ff:].T,
        total[3],
        total[4],
        total[5],
        g_pw,
        jnp.sum(z_all, 0),
        g_cw,
        jnp.sum(d_all, 0),
    )


def solution(mesh):
    rep = P()
    seq = P("dp", None, None)
    col = P("tensor")
    wide = P("dp", None, "tensor")
    up = P("dp", "tensor")
    down = P("tensor", "dp")
    return jax.shard_map(
        local,
        mesh=mesh,
        in_specs=(seq, seq, P("dp"), P("dp"), wide, col, col, down, rep, rep, rep, up, col, down)
        + (rep,) * 7,
        out_specs=(seq, seq, rep, wide, col, col, down, rep, rep, rep, up, col, down)
        + (rep,) * 7,
        check_vma=False,
    )
```
